32 devices in a mesh: groups: 2 (over y), tok: 16 (over z, x, core).
Axes of the slice: x: 2, y: 2, z: 4, core: 2. Of those that a mesh axis runs over, the one named last changes fastest.
Arguments:
- queries: bfloat16 [1024, 2048], P(('groups', 'tok')), parts along dimension 0, may hold values from -6 to 6
- new_kv: bfloat16 [3072, 4096], P(('groups', 'tok')), parts along dimension 0, may hold values from -6 to 6
- prev_kv: bfloat16 [2, 3072, 4096], P(None, ('groups', 'tok')), parts along dimension 1, may hold values from -6 to 6
- base_step: int32 [32], P(('groups', 'tok')), parts along dimension 0, may hold values from 0 to 1
- live_counts: int32 [32], P('groups'), parts along dimension 0, may hold values from 1 to 96
- sketch: float32 [4096, 32], replicated, may hold values from -0.09375 to 0.09375
- cache: bfloat16 [64, 1536, 128], P(('groups', 'tok')), parts along dimension 0, may hold values from -6 to 6, as said below
- w_out: bfloat16 [2048, 1536], replicated, may hold values from -0.125 to 0.125
Outputs:
- projected: bfloat16 [1024, 1536], P(('groups', 'tok')), parts along dimension 0
The draws below stay inside these ranges and needn't reach their ends.
There are 2 independent parts, one for each index of `groups`. The reference program is written for one: setup_inputs(seed, part) draws one part's arguments, and reference() takes and returns one part's arrays. A program takes and returns all parts, laid end to end along the dimension named above; an argument that names none is the same for every part. Nothing has to cross between parts.
Inputs may be any that keep to these rules, and one draw needn't show every extreme that they name: cache slots i and j hold the same values when i // 2 == j // 2 and i % 2 == j % 2.
All inputs are finite; a program needn't handle non-finite values.
Results may differ from the reference program's by a relative error of at most 0.019.
Values may be sent and summed in bfloat16 or wider, within the bound.
No kernel may reach another device: no remote copies, remote signals or barrier semaphores. Data moves between devices by JAX's collectives and lax.ppermute only.
A program may use at most 128 MiB of HBM per device.

```python
import math
import jax
import jax.numpy as jnp
import numpy as np
from jax import lax

HEADS = 32
HD = 64
D_OUT = 1536
R = 32
SWEEPS = 2
HIST = 2
TOK_DEV = 96
SHARDS = 16
KEYS = 1536
QROWS = 512
HH = 2048
QG = 1
HPD = 2


def draw_cache(key, part):
    base_draw = jnp.clip(jax.random.normal(jax.random.fold_in(key, 12), (HEADS, KEYS, 2 * HD), jnp.float32), -6.0, 6.0)
    slot_ids = np.arange(SHARDS * HPD)
    head_of_row = slot_ids // HPD // QG * HPD + slot_ids % HPD
    return base_draw[head_of_row].astype(jnp.bfloat16)


def draw_queries(key, part):
    query_draw = jnp.clip(jax.random.normal(jax.random.fold_in(key, 13), (QROWS, HH), jnp.float32), -6.0, 6.0)
    return query_draw.astype(jnp.bfloat16)


def draw_live_counts(key, part):
    counts = jax.random.randint(jax.random.fold_in(key, 3), (SHARDS,), 1, TOK_DEV + 1)
    full_shard = jax.random.randint(jax.random.fold_in(key, 4), (), 0, SHARDS)
    return jnp.where(jnp.arange(SHARDS) == full_shard, TOK_DEV, counts).astype(jnp.int32)


def touch_ends(values, key, least, high):
    longest = values.shape.index(max(values.shape))
    spots = []
    for shift in (0, 1):
        where = [jax.random.randint(jax.random.fold_in(key, axis), (), 0, length) for axis, length in enumerate(values.shape)]
        where[longest] = (where[longest] + shift) % values.shape[longest]
        spots.append(tuple(where))
    return values.at[spots[0]].set(least).at[spots[1]].set(high)


def levels(stream_key, dims, cuts, low, top_value):
    factor_of = 1.0
    for dim, blocks in cuts:
        steps = jax.random.uniform(jax.random.fold_in(jax.random.fold_in(stream_key, 6), dim), (blocks,), jnp.float32, low / len(cuts), top_value / len(cuts))
        factor_of = factor_of * jnp.repeat(jnp.exp(steps), dims[dim] // blocks).reshape((-1,) + (1,) * (len(dims) - 1 - dim))
    return factor_of


def centred(rng, extent, width, most, cuts=(), kind=jnp.bfloat16):
    result = jax.random.normal(rng, extent, jnp.float32) * width
    if len(cuts) > 0:
        result = levels(rng, extent, cuts, -0.22, 0.18) * result
    return jnp.clip(result, min=-most, max=most).astype(kind)


def setup_inputs(seed: int = 0, part: int = 0) -> dict:
    splits = jax.random.split(jax.random.key(seed), 9)
    part_keys = jax.random.split(jax.random.fold_in(splits[8], part), 9)
    queries = draw_queries(jax.random.fold_in(jax.random.fold_in(splits[8], part), 71), part)
    new_kv = centred(part_keys[1], (KEYS, 2 * HH), 1.0, 6.0, ((0, 16),))
    prev_kv = centred(part_keys[2], (HIST, KEYS, 2 * HH), 1.0, 6.0, ((1, 16),))
    base_step = touch_ends(jax.random.randint(part_keys[3], (SHARDS,), 0, HIST), jax.random.fold_in(part_keys[3], 1), 0, HIST - 1).astype(jnp.int32)
    live_counts = draw_live_counts(jax.random.fold_in(jax.random.fold_in(splits[8], part), 71), part)
    sketch = centred(splits[5], (2 * HH, R), (2 * HH) ** -0.5, 0.09375, (), jnp.float32)
    cache = draw_cache(jax.random.fold_in(jax.random.fold_in(splits[8], part), 71), part)
    w_out = centred(splits[7], (HH, D_OUT), HH ** -0.5, 0.125)
    return dict(queries=queries, new_kv=new_kv, prev_kv=prev_kv, base_step=base_step, live_counts=live_counts, sketch=sketch, cache=cache, w_out=w_out)


highest = lax.Precision.HIGHEST

def orthonormal(block_cols):
    gram_matrix = jnp.dot(block_cols.T, block_cols, precision=highest)
    lower_factor = jnp.linalg.cholesky(gram_matrix)
    return jax.scipy.linalg.solve_triangular(lower_factor, block_cols.T, lower=True).T

def compress(delta_block, sketch):
    basis_cols = orthonormal(jnp.dot(delta_block, sketch, precision=highest))
    for sweep_index in range(SWEEPS):
        inner = jnp.dot(delta_block.T, basis_cols, precision=highest)
        basis_cols = orthonormal(jnp.dot(delta_block, inner, precision=highest))
    right_factor = jnp.dot(basis_cols.T, delta_block, precision=highest)
    return (basis_cols.astype(jnp.bfloat16), right_factor.astype(jnp.bfloat16))

def reference(queries, new_kv, prev_kv, base_step, live_counts, sketch, cache, w_out):
    prev_blocks = prev_kv.reshape(HIST, SHARDS, TOK_DEV, 2 * HH)
    prior = prev_blocks[0].astype(jnp.float32)
    for history in range(1, HIST):
        prior = jnp.where((base_step == history)[:, None, None], prev_blocks[history].astype(jnp.float32), prior)
    delta = new_kv.astype(jnp.float32).reshape(SHARDS, TOK_DEV, 2 * HH) - prior
    left_factor, right_factor = lax.map(lambda delta_block: compress(delta_block, sketch), delta)
    lowrank = jnp.einsum('str,src->stc', left_factor.astype(jnp.float32), right_factor.astype(jnp.float32))
    lowrank = lowrank.astype(jnp.bfloat16).reshape(KEYS, HEADS, 2 * HD).transpose(1, 0, 2)
    copy_index = np.array([head_id // HPD * QG * HPD + head_id % HPD for head_id in range(HEADS)], dtype=np.int32)
    cache_heads = cache[copy_index]
    live_keys = (jnp.arange(TOK_DEV, dtype=jnp.int32)[None, :] < live_counts[:, None]).reshape(KEYS)
    q_heads = queries.reshape(QROWS, HEADS, HD).transpose(1, 0, 2)
    block_rows = math.gcd(QROWS, 512)

    def one_head(pieces):
        q_head, cache_head, low_head = pieces
        keys_values = (cache_head.astype(jnp.float32) + low_head.astype(jnp.float32)).astype(jnp.bfloat16)
        key_part = keys_values[:, :HD]
        value_part = keys_values[:, HD:]

        def one_block(query_block):
            scores = jnp.dot(query_block.astype(jnp.float32), key_part.T.astype(jnp.float32), preferred_element_type=jnp.float32) * HD ** (-0.5)
            scores = jnp.where(live_keys[None, :], scores, -1e+30)
            row_max = jnp.max(scores, axis=-1, keepdims=True)
            exponent = jnp.exp(scores - row_max)
            weights = (exponent / jnp.sum(exponent, axis=-1, keepdims=True)).astype(jnp.bfloat16)
            return jnp.dot(weights.astype(jnp.float32), value_part.astype(jnp.float32), preferred_element_type=jnp.float32).astype(jnp.bfloat16)
        return lax.map(one_block, q_head.reshape(QROWS // block_rows, block_rows, HD)).reshape(QROWS, HD)
    attended = lax.map(one_head, (q_heads, cache_heads, lowrank))
    attended = attended.transpose(1, 0, 2).reshape(QROWS, HH)
    return jnp.dot(attended.astype(jnp.float32), w_out.astype(jnp.float32), preferred_element_type=jnp.float32).astype(jnp.bfloat16)
```

```python
import functools
import math

import jax
import jax.numpy as jnp
from jax import lax
from jax.experimental import pallas as pl
from jax.experimental.pallas import tpu as pltpu
from jax.sharding import PartitionSpec as P

HD = 64
SWEEPS = 2
LANES = 128
NT = (((1,), (1,)), ((), ()))
NN = (((1,), (0,)), ((), ()))
highest = lax.Precision.HIGHEST
f32 = jnp.float32
bf16 = jnp.bfloat16


def up(value, to):
    return -(-value // to) * to


def matmul(a, b, dims, precision=None):
    return lax.dot_general(a, b, dims, precision=precision, preferred_element_type=f32)


def split(x):
    high = x.astype(bf16)
    return high, (x - high.astype(f32)).astype(bf16)


def eliminate(m, cols, width):
    rank = m.shape[0]
    row_id = lax.broadcasted_iota(jnp.int32, m.shape, 0)
    scale = jnp.zeros_like(m)
    for start in range(0, rank, width):
        col = [jnp.broadcast_to(m[:, cols + start + k : cols + start + k + 1], m.shape) for k in range(width)]
        row = [jnp.broadcast_to(m[start + k : start + k + 1, :], (8, m.shape[1])) for k in range(width)]
        cell = [
            [jnp.broadcast_to(col[b][start + a : start + a + 1, :], (8, m.shape[1])) for b in range(a + 1)]
            for a in range(width)
        ]
        for k in range(width):
            inverse = 1.0 / cell[k][k]
            times = {a: cell[a][k] * inverse for a in range(k + 1, width)}
            tall = lambda x: jnp.concatenate([x] * (rank // 8), axis=0)
            below = jnp.where(row_id > start + k, col[k], 0.0) * tall(inverse)
            m = m - below * tall(row[k])
            scale = jnp.where(row_id == start + k, tall(cell[k][k]), scale)
            for a in range(k + 1, width):
                for b in range(k + 1, a + 1):
                    cell[a][b] = cell[a][b] - times[a] * cell[b][k]
                row[a] = row[a] - times[a] * row[k]
                col[a] = col[a] - tall(times[a]) * col[k]
    return m * lax.rsqrt(scale)


def compress_kernel(
    plan,
    base_ref,
    live_ref,
    new_ref,
    prev_ref,
    sketch_ref,
    q_ref,
    cache_ref,
    w_ref,
    out_ref,
    limits_ref,
    cache_out,
    w_out,
    new_buf,
    prev_buf,
    sketch_buf,
    q_buf,
    live_buf,
    terms,
    new_sems,
    prev_sems,
    sketch_sems,
    sems,
):
    tokens, columns = new_ref.shape
    rank = sketch_ref.shape[0]
    chunks = new_buf.shape[0]
    step = columns // chunks
    gap = up(tokens, LANES)
    per_dev, parts, part_rows, q_at, left_at = plan
    receivers = out_ref.shape[0]
    groups = receivers // parts
    base = jnp.where(base_ref[0] == 1, 1, 0)
    copies = []
    for c in range(chunks):
        at = pl.ds(c * step, step)
        trio = (
            pltpu.make_async_copy(new_ref.at[:, at], new_buf.at[c], new_sems.at[c]),
            pltpu.make_async_copy(prev_ref.at[base, :, at], prev_buf.at[c], prev_sems.at[c]),
            pltpu.make_async_copy(sketch_ref.at[:, at], sketch_buf.at[c], sketch_sems.at[c]),
        )
        for copy in trio:
            copy.start()
        copies.append(trio)
    q_copy = pltpu.make_async_copy(q_ref, q_buf, sems.at[0])
    live_copy = pltpu.make_async_copy(live_ref, live_buf, sems.at[1])
    later = (
        pltpu.make_async_copy(cache_ref, cache_out, sems.at[2]),
        pltpu.make_async_copy(w_ref, w_out, sems.at[3]),
    )
    for copy in (q_copy, live_copy) + later:
        copy.start()

    if gap > tokens:
        terms[tokens:gap, :] = jnp.zeros((gap - tokens, columns), bf16)
    total = jnp.zeros((tokens + 2 * rank, gap + tokens), f32)
    for c in range(chunks):
        at = slice(c * step, (c + 1) * step)
        for copy in copies[c]:
            copy.wait()
        delta = new_buf[c].astype(f32) - prev_buf[c].astype(f32)
        high, low = split(delta)
        terms[0:tokens, at] = high
        terms[gap : gap + tokens, at] = low
        s_high, s_low = split(sketch_buf[c])
        total = total + matmul(jnp.concatenate([high, s_high, s_low], axis=0), terms[:, at], NT)
    q_copy.wait()
    for g in range(groups):
        for j in range(parts):
            if q_buf.ndim == 2:
                block = q_buf[j * part_rows : (j + 1) * part_rows, g * LANES : (g + 1) * LANES]
            else:
                block = q_buf[g * parts + j]
            out_ref[g * parts + j, q_at : q_at + block.shape[0], :] = block

    live_copy.wait()
    for s in range(receivers):
        limits_ref[s : s + 1, :] = jnp.full((1, LANES), live_buf[s], jnp.int32)

    cross = total[:tokens, gap:]
    gram = total[:tokens, :tokens] + cross + cross.T
    sketched = total[tokens : tokens + rank]
    y = sketched[:, :tokens] + sketched[:, gap:] + total[tokens + rank :, :tokens]

    eye = jnp.where(
        lax.broadcasted_iota(jnp.int32, (tokens, tokens), 0) == lax.broadcasted_iota(jnp.int32, (tokens, tokens), 1),
        1.0,
        0.0,
    )
    for sweep in range(SWEEPS + 1):
        if sweep:
            y = matmul(basis, gram, NN, highest)
        both = matmul(y, jnp.concatenate([eye, y], axis=0), NT, highest)
        basis = eliminate(both, tokens, 4)[:, :tokens]

    high, low = split(basis)
    blank = jnp.zeros((rank, gap - tokens), bf16)
    first = jnp.concatenate([high, blank, high] if gap > tokens else [high, high], axis=1)
    second = jnp.concatenate([low, jnp.zeros((rank, gap), bf16)], axis=1)
    lhs = jnp.concatenate([first, second], axis=0)

    blocks = LANES // rank
    packed_rows = tokens // blocks
    tiled = jnp.concatenate([high] * blocks, axis=0)
    lane = lax.broadcasted_iota(jnp.int32, (packed_rows, LANES), 1)
    packed = jnp.zeros((packed_rows, LANES), f32)
    for k in range(blocks):
        pick = (
            lax.broadcasted_iota(jnp.int32, (packed_rows, tokens), 1)
            == lax.broadcasted_iota(jnp.int32, (packed_rows, tokens), 0) + k * packed_rows
        )
        packed = jnp.where(lane // rank == k, matmul(jnp.where(pick, 1.0, 0.0).astype(bf16), tiled, NT), packed)
    packed = packed.astype(bf16)

    width = 2 * HD
    for g in range(groups):
        for d in range(per_dev):
            head = g * per_dev + d
            pair = matmul(lhs, terms[:, head * width : (head + 1) * width], NN)
            block = (pair[:rank] + pair[rank:]).astype(bf16)
            for j in range(parts):
                out_ref[g * parts + j, d * rank : (d + 1) * rank, :] = block
        for j in range(parts):
            out_ref[g * parts + j, left_at : left_at + packed_rows, :] = packed
    for copy in later:
        copy.wait()


def attend_kernel(plan, block_rows, limits_ref, got_ref, cache_ref, out_ref, keys, values, q_all):
    per_dev, part_rows, rank, tokens, q_at, left_at = plan
    shards = got_ref.shape[0]
    blocks = LANES // rank
    packed_rows = tokens // blocks
    lane_p = lax.broadcasted_iota(jnp.int32, (packed_rows, LANES), 1)
    lane_t = lax.broadcasted_iota(jnp.int32, (tokens, LANES), 1)
    row_t = lax.broadcasted_iota(jnp.int32, (tokens, LANES), 0)

    def one_shard(s, carry):
        packed = got_ref[s, left_at : left_at + packed_rows, :].astype(f32)
        left = jnp.concatenate([jnp.where(lane_p // rank == k, packed, 0.0) for k in range(blocks)], axis=0).astype(bf16)
        at = pl.ds(pl.multiple_of(s * tokens, tokens), tokens)
        dead = jnp.where((lane_t == HD) & (row_t >= limits_ref[pl.ds(s, 1), :]), -1e30, 0.0)
        right = jnp.concatenate([got_ref[s, d * rank : (d + 1) * rank, :] for d in range(per_dev)], axis=1)
        lowrank = matmul(left, jnp.concatenate([right] * blocks, axis=0), NN).astype(bf16)
        for d in range(per_dev):
            both = cache_ref[d, at, :].astype(f32) + lowrank[:, d * LANES : (d + 1) * LANES].astype(f32)
            keys[d, at, :] = jnp.where(lane_t < HD, both, dead).astype(bf16)
            values[d, at, :] = jnp.where(lane_t < HD, 1.0, both).astype(bf16)
        return carry

    lax.fori_loop(0, shards, one_shard, 0, unroll=math.gcd(shards, 16))

    padded = got_ref[:, q_at : q_at + up(part_rows, 16), :].astype(f32)
    q_rows = padded[:, :part_rows, :].reshape(shards * part_rows, LANES)
    lane_q = lax.broadcasted_iota(jnp.int32, q_rows.shape, 1)
    for d in range(per_dev):
        moved = q_rows if d == 0 else pltpu.roll(q_rows, LANES - d * HD, 1)
        q_all[d] = jnp.where(lane_q < HD, moved * HD**-0.5, jnp.where(lane_q == HD, 1.0, 0.0)).astype(bf16)

    lane_o = lax.broadcasted_iota(jnp.int32, (block_rows, LANES), 1)

    def one_block(b, carry):
        at = pl.ds(pl.multiple_of(b * block_rows, block_rows), block_rows)
        out = jnp.zeros((block_rows, LANES), f32)
        for d in range(per_dev):
            scores = matmul(q_all[d, at, :], keys[d], NT)
            exponent = jnp.exp(scores - jnp.max(scores, axis=1, keepdims=True)).astype(bf16)
            sums = matmul(exponent, values[d], NN)
            flipped = pltpu.roll(sums, HD, 1)
            if d == 0:
                out = flipped / sums
            else:
                out = jnp.where(lane_o < HD, out, sums / flipped)
        out_ref[at, :] = out.astype(bf16)
        return carry

    count = shards * part_rows // block_rows
    if count == 1:
        one_block(0, 0)
    else:
        lax.fori_loop(0, count, one_block, 0)


def project_kernel(x_ref, w_ref, out_ref, buf, sems):
    chunks, rows, step = buf.shape
    copies = []
    for c in range(chunks):
        at = slice(c * step, (c + 1) * step)
        buf[c] = matmul(x_ref[...], w_ref[:, at], NN).astype(bf16)
        copies.append(pltpu.make_async_copy(buf.at[c], out_ref.at[:, pl.ds(c * step, step)], sems.at[c]))
        copies[c].start()
    for copy in copies:
        copy.wait()


def per_device(queries, new_kv, prev_kv, base_step, live_counts, sketch, cache, w_out):
    shards = lax.axis_size("tok")
    tokens, columns = new_kv.shape
    rank = sketch.shape[1]
    query_rows = queries.shape[0]
    head_count = queries.shape[1] // HD
    parts = max(1, shards // head_count)
    per_dev = head_count * parts // shards
    groups = head_count // per_dev
    part_rows = query_rows // parts
    key_count = shards * tokens
    query_count = shards * part_rows
    q_width = per_dev * HD

    q_at = per_dev * rank
    left_at = q_at + up(part_rows, 16)
    rows = left_at + tokens * rank // LANES
    if q_width == LANES and part_rows % 16 == 0:
        q_in = queries
    else:
        q_in = queries.reshape(parts, part_rows, groups, q_width).transpose(2, 0, 1, 3)
        q_in = q_in.reshape(shards, part_rows, q_width)
        q_in = jnp.pad(q_in, ((0, 0), (0, up(part_rows, 16) - part_rows), (0, LANES - q_width)))

    vmem = pl.BlockSpec(memory_space=pltpu.VMEM)
    smem = pl.BlockSpec(memory_space=pltpu.SMEM)
    chunks = 4
    step = columns // chunks
    hbm = pl.BlockSpec(memory_space=pltpu.HBM)
    inputs = (live_counts, new_kv, prev_kv, sketch.T, q_in, cache, w_out)
    inputs = [pltpu.with_memory_space_constraint(x, pltpu.HBM) for x in inputs]
    send, limits, cache, w_out = pl.pallas_call(
        functools.partial(compress_kernel, (per_dev, parts, part_rows, q_at, left_at)),
        out_shape=(
            jax.ShapeDtypeStruct((shards, rows, LANES), bf16),
            jax.ShapeDtypeStruct((shards, LANES), jnp.int32),
            jax.ShapeDtypeStruct(cache.shape, bf16),
            jax.ShapeDtypeStruct(w_out.shape, bf16),
        ),
        in_specs=[smem] + [hbm] * 7,
        out_specs=(vmem,) * 4,
        scratch_shapes=[
            pltpu.VMEM((chunks, tokens, step), bf16),
            pltpu.VMEM((chunks, tokens, step), bf16),
            pltpu.VMEM((chunks, rank, step), f32),
            pltpu.VMEM(q_in.shape, bf16),
            pltpu.SMEM((shards,), jnp.int32),
            pltpu.VMEM((up(tokens, LANES) + tokens, columns), bf16),
            pltpu.SemaphoreType.DMA((chunks,)),
            pltpu.SemaphoreType.DMA((chunks,)),
            pltpu.SemaphoreType.DMA((chunks,)),
            pltpu.SemaphoreType.DMA((4,)),
        ],
        compiler_params=pltpu.CompilerParams(vmem_limit_bytes=20 << 20),
        name="compress",
    )(base_step, *inputs)

    got = lax.all_to_all(send, "tok", split_axis=0, concat_axis=0, tiled=True)

    block_rows = query_count
    while block_rows * key_count * 4 > (4 << 20):
        block_rows //= 2
    attended = pl.pallas_call(
        functools.partial(attend_kernel, (per_dev, part_rows, rank, tokens, q_at, left_at), block_rows),
        out_shape=jax.ShapeDtypeStruct((query_count, LANES), bf16),
        in_specs=[vmem, vmem, vmem],
        out_specs=vmem,
        scratch_shapes=[
            pltpu.VMEM((per_dev, key_count, LANES), bf16),
            pltpu.VMEM((per_dev, key_count, LANES), bf16),
            pltpu.VMEM((per_dev, query_count, LANES), bf16),
        ],
        compiler_params=pltpu.CompilerParams(vmem_limit_bytes=32 << 20),
        name="attend",
    )(limits, got, cache)
    attended = attended.reshape(shards, part_rows, LANES)[:, :, :q_width]

    returned = lax.all_to_all(attended, "tok", split_axis=0, concat_axis=0, tiled=True)
    returned = returned.reshape(groups, parts, part_rows, q_width)
    row_block = returned.transpose(1, 2, 0, 3).reshape(query_rows, head_count * HD)
    chunks = 2
    return pl.pallas_call(
        project_kernel,
        out_shape=jax.ShapeDtypeStruct((query_rows, w_out.shape[1]), bf16),
        in_specs=[vmem, vmem],
        out_specs=hbm,
        scratch_shapes=[
            pltpu.VMEM((chunks, query_rows, w_out.shape[1] // chunks), bf16),
            pltpu.SemaphoreType.DMA((chunks,)),
        ],
        compiler_params=pltpu.CompilerParams(vmem_limit_bytes=8 << 20),
        name="project",
    )(row_block, w_out)


def solution(mesh):
    return jax.shard_map(
        per_device,
        mesh=mesh,
        in_specs=(
            P(("groups", "tok"), None),
            P(("groups", "tok"), None),
            P(None, ("groups", "tok"), None),
            P(("groups", "tok")),
            P("groups"),
            P(),
            P(("groups", "tok"), None, None),
            P(),
        ),
        out_specs=P(("groups", "tok"), None),
        check_vma=False,
    )
```

```python
import functools
import math

import jax
import jax.numpy as jnp
from jax import lax
from jax.experimental import pallas as pl
from jax.experimental.pallas import tpu as pltpu
from jax.sharding import PartitionSpec as P

HD = 64
SWEEPS = 2
LANES = 128
NT = (((1,), (1,)), ((), ()))
NN = (((1,), (0,)), ((), ()))
highest = lax.Precision.HIGHEST
f32 = jnp.float32
bf16 = jnp.bfloat16


def up(value, to):
    return -(-value // to) * to


def matmul(a, b, dims, precision=None):
    return lax.dot_general(a, b, dims, precision=precision, preferred_element_type=f32)


def split(x):
    high = x.astype(bf16)
    return high, (x - high.astype(f32)).astype(bf16)


def eliminate(m, cols):
    rank, wide = m.shape
    tile = 8
    rest = [m[i : i + tile] for i in range(0, rank, tile)]
    row_id = lax.broadcasted_iota(jnp.int32, (tile, wide), 0)
    spread = lambda x, i: jnp.broadcast_to(x[i : i + 1], (tile, wide))
    done = []
    for start in range(0, rank, tile):
        lane = [jnp.full((tile, wide), cols + start + k, jnp.int32) for k in range(tile)]
        col = [[jnp.take_along_axis(r, at, axis=1, mode="promise_in_bounds") for r in rest] for at in lane]
        row = [spread(rest[0], k) for k in range(tile)]
        head = jnp.zeros((tile, wide), f32)
        pivot = spread(col[0][0], 0)
        for k in range(tile):
            later = range(k + 1, tile)
            ahead = {a: spread(col[a][0], k) for a in later}
            following = spread(col[k + 1][0], k + 1) if k + 1 < tile else None
            root = lax.rsqrt(pivot)
            times = {a: ahead[a] * root for a in later}
            if k + 1 < tile:
                pivot = following - times[k + 1] * times[k + 1]
            row[k] = row[k] * root
            head = jnp.where(row_id == k, row[k], head)
            below = [c * root for c in col[k]]
            for a in later:
                row[a] = row[a] - times[a] * row[k]
                col[a] = [c - times[a] * d for c, d in zip(col[a], below)]
            for i in range(1, len(rest)):
                rest[i] = rest[i] - below[i] * row[k]
        done.append(head)
        rest = rest[1:]
    return jnp.concatenate(done, axis=0)


def compress_kernel(
    plan,
    base_ref,
    live_ref,
    new_ref,
    prev_ref,
    sketch_ref,
    q_ref,
    cache_ref,
    w_ref,
    out_ref,
    dead_ref,
    cache_out,
    w_out,
    new_buf,
    prev_buf,
    sketch_buf,
    q_buf,
    live_buf,
    terms,
    new_sems,
    prev_sems,
    sketch_sems,
    sems,
):
    tokens, columns = new_ref.shape
    rank = sketch_ref.shape[0]
    chunks = new_buf.shape[0]
    step = columns // chunks
    per_dev, parts, part_rows, q_at, left_at = plan
    receivers = out_ref.shape[0]
    groups = receivers // parts
    base = jnp.where(base_ref[0] == 1, 1, 0)
    q_copy = pltpu.make_async_copy(q_ref, q_buf, sems.at[0])
    live_copy = pltpu.make_async_copy(live_ref, live_buf, sems.at[1])
    live_copy.start()
    q_copy.start()
    copies = []
    for c in range(chunks):
        at = pl.ds(c * step, step)
        trio = (
            pltpu.make_async_copy(new_ref.at[:, at], new_buf.at[c], new_sems.at[c]),
            pltpu.make_async_copy(prev_ref.at[base, :, at], prev_buf.at[c], prev_sems.at[c]),
            pltpu.make_async_copy(sketch_ref.at[:, at], sketch_buf.at[c], sketch_sems.at[c]),
        )
        for copy in trio:
            copy.start()
        copies.append(trio)
    later = (
        pltpu.make_async_copy(cache_ref, cache_out, sems.at[2]),
        pltpu.make_async_copy(w_ref, w_out, sems.at[3]),
    )
    for copy in later:
        copy.start()

    live_copy.wait()
    row_t = lax.broadcasted_iota(jnp.int32, (tokens, LANES), 0)
    lane_t = lax.broadcasted_iota(jnp.int32, (tokens, LANES), 1)
    edge = jnp.where(lane_t == HD, row_t, -1)
    for s in range(receivers):
        dead_ref[s] = jnp.where(edge >= live_buf[s], -1e30, 0.0).astype(bf16)
    q_copy.wait()
    for g in range(groups):
        for j in range(parts):
            if q_buf.ndim == 2:
                block = q_buf[j * part_rows : (j + 1) * part_rows, g * LANES : (g + 1) * LANES]
            else:
                block = q_buf[g * parts + j]
            out_ref[g * parts + j, q_at : q_at + block.shape[0], :] = block * bf16(HD**-0.5)

    both_sums = [jnp.zeros((tokens + 2 * rank, 2 * tokens), f32)] * 2
    for c in range(chunks):
        at = slice(c * step, (c + 1) * step)
        for copy in copies[c]:
            copy.wait()
        delta = new_buf[c].astype(f32) - prev_buf[c].astype(f32)
        high, low = split(delta)
        terms[:, at] = high
        s_high, s_low = split(sketch_buf[c])
        lhs = jnp.concatenate([high, s_high, s_low], axis=0)
        rhs = jnp.concatenate([high, low], axis=0)
        for k in range(0, step, 256):
            both_sums[(k // 256) % 2] = both_sums[(k // 256) % 2] + matmul(lhs[:, k : k + 256], rhs[:, k : k + 256], NT)
    sums = both_sums[0] + both_sums[1]
    total, cross = sums[:, :tokens], sums[:, tokens:]
    gram = total[:tokens] + cross[:tokens] + cross[:tokens].T
    y = total[tokens : tokens + rank] + total[tokens + rank :] + cross[tokens : tokens + rank]

    eye = jnp.where(
        lax.broadcasted_iota(jnp.int32, (tokens, tokens), 0) == lax.broadcasted_iota(jnp.int32, (tokens, tokens), 1),
        1.0,
        0.0,
    )
    for sweep in range(SWEEPS + 1):
        if sweep:
            y = matmul(basis, gram, NN, highest)
        both = matmul(y, jnp.concatenate([eye, y], axis=0), NT, highest)
        basis = eliminate(both, tokens)[:, :tokens]

    high, low = split(basis)
    lhs = jnp.concatenate([high, low], axis=0)

    blocks = LANES // rank
    packed_rows = tokens // blocks
    tiled = jnp.concatenate([high] * blocks, axis=0)
    lane = lax.broadcasted_iota(jnp.int32, (packed_rows, LANES), 1)
    packed = jnp.zeros((packed_rows, LANES), f32)
    for k in range(blocks):
        pick = (
            lax.broadcasted_iota(jnp.int32, (packed_rows, tokens), 1)
            == lax.broadcasted_iota(jnp.int32, (packed_rows, tokens), 0) + k * packed_rows
        )
        packed = jnp.where(lane // rank == k, matmul(jnp.where(pick, 1.0, 0.0).astype(bf16), tiled, NT), packed)
    packed = packed.astype(bf16)

    width = 2 * HD * per_dev
    for g in range(groups):
        pair = matmul(lhs, terms[:, g * width : (g + 1) * width], NN)
        block = (pair[:rank] + pair[rank:]).astype(bf16)
        for j in range(parts):
            for d in range(per_dev):
                out_ref[g * parts + j, d * rank : (d + 1) * rank, :] = block[:, d * LANES : (d + 1) * LANES]
            out_ref[g * parts + j, left_at : left_at + packed_rows, :] = packed
    for copy in later:
        copy.wait()


def attend_kernel(plan, block_rows, dead_ref, got_ref, cache_ref, out_ref, keys, values, q_all):
    per_dev, part_rows, rank, tokens, q_at, left_at = plan
    shards = got_ref.shape[0]
    blocks = LANES // rank
    packed_rows = tokens // blocks
    lane_p = lax.broadcasted_iota(jnp.int32, (packed_rows, LANES), 1)
    is_key = lax.broadcasted_iota(jnp.int32, (tokens, LANES), 1) < HD
    ones = jnp.ones((tokens, LANES), bf16)

    def one_shard(s, carry):
        packed = got_ref[s, left_at : left_at + packed_rows, :].astype(f32)
        left = jnp.concatenate([jnp.where(lane_p // rank == k, packed, 0.0) for k in range(blocks)], axis=0).astype(bf16)
        at = pl.ds(pl.multiple_of(s * tokens, tokens), tokens)
        right = jnp.concatenate([got_ref[s, d * rank : (d + 1) * rank, :] for d in range(per_dev)], axis=1)
        lowrank = matmul(left, jnp.concatenate([right] * blocks, axis=0), NN).astype(bf16)
        for d in range(per_dev):
            both = cache_ref[d, at, :] + lowrank[:, d * LANES : (d + 1) * LANES]
            keys[d, at, :] = jnp.where(is_key, both, dead_ref[s])
            values[d, at, :] = jnp.where(is_key, ones, both)
        return carry

    lax.fori_loop(0, shards, one_shard, 0, unroll=math.gcd(shards, 16))

    padded = got_ref[:, q_at : q_at + up(part_rows, 16), :].astype(f32)
    q_rows = padded[:, :part_rows, :].reshape(shards * part_rows, LANES)
    lane_q = lax.broadcasted_iota(jnp.int32, q_rows.shape, 1)
    for d in range(per_dev):
        moved = q_rows if d == 0 else pltpu.roll(q_rows, LANES - d * HD, 1)
        q_all[d] = jnp.where(lane_q < HD, moved, jnp.where(lane_q == HD, 1.0, 0.0)).astype(bf16)

    lane_o = lax.broadcasted_iota(jnp.int32, (block_rows, LANES), 1)

    def one_block(b, carry):
        at = pl.ds(pl.multiple_of(b * block_rows, block_rows), block_rows)
        out = jnp.zeros((block_rows, LANES), f32)
        for d in range(per_dev):
            scores = matmul(q_all[d, at, :], keys[d], NT)
            exponent = jnp.exp(scores - jnp.max(scores, axis=1, keepdims=True)).astype(bf16)
            sums = matmul(exponent, values[d], NN)
            flipped = pltpu.roll(sums, HD, 1)
            if d == 0:
                out = flipped / sums
            else:
                out = jnp.where(lane_o < HD, out, sums / flipped)
        out_ref[at, :] = out.astype(bf16)
        return carry

    count = shards * part_rows // block_rows
    if count == 1:
        one_block(0, 0)
    else:
        lax.fori_loop(0, count, one_block, 0)


def project_kernel(x_ref, w_ref, out_ref, buf, sems):
    chunks, rows, step = buf.shape
    copies = []
    for c in range(chunks):
        at = slice(c * step, (c + 1) * step)
        buf[c] = matmul(x_ref[...], w_ref[:, at], NN).astype(bf16)
        copies.append(pltpu.make_async_copy(buf.at[c], out_ref.at[:, pl.ds(c * step, step)], sems.at[c]))
        copies[c].start()
    for copy in copies:
        copy.wait()


def per_device(queries, new_kv, prev_kv, base_step, live_counts, sketch, cache, w_out):
    shards = lax.axis_size("tok")
    tokens, columns = new_kv.shape
    rank = sketch.shape[1]
    query_rows = queries.shape[0]
    head_count = queries.shape[1] // HD
    parts = max(1, shards // head_count)
    per_dev = head_count * parts // shards
    groups = head_count // per_dev
    part_rows = query_rows // parts
    key_count = shards * tokens
    query_count = shards * part_rows
    q_width = per_dev * HD

    q_at = per_dev * rank
    left_at = q_at + up(part_rows, 16)
    rows = left_at + tokens * rank // LANES
    if q_width == LANES and part_rows % 16 == 0:
        q_in = queries
    else:
        q_in = queries.reshape(parts, part_rows, groups, q_width).transpose(2, 0, 1, 3)
        q_in = q_in.reshape(shards, part_rows, q_width)
        q_in = jnp.pad(q_in, ((0, 0), (0, up(part_rows, 16) - part_rows), (0, LANES - q_width)))

    vmem = pl.BlockSpec(memory_space=pltpu.VMEM)
    smem = pl.BlockSpec(memory_space=pltpu.SMEM)
    chunks = 4
    step = columns // chunks
    hbm = pl.BlockSpec(memory_space=pltpu.HBM)
    inputs = (live_counts, new_kv, prev_kv, sketch.T, q_in, cache, w_out)
    inputs = [pltpu.with_memory_space_constraint(x, pltpu.HBM) for x in inputs]
    send, dead, cache, w_out = pl.pallas_call(
        functools.partial(compress_kernel, (per_dev, parts, part_rows, q_at, left_at)),
        out_shape=(
            jax.ShapeDtypeStruct((shards, rows, LANES), bf16),
            jax.ShapeDtypeStruct((shards, tokens, LANES), bf16),
            jax.ShapeDtypeStruct(cache.shape, bf16),
            jax.ShapeDtypeStruct(w_out.shape, bf16),
        ),
        in_specs=[smem] + [hbm] * 7,
        out_specs=(vmem,) * 4,
        scratch_shapes=[
            pltpu.VMEM((chunks, tokens, step), bf16),
            pltpu.VMEM((chunks, tokens, step), bf16),
            pltpu.VMEM((chunks, rank, step), f32),
            pltpu.VMEM(q_in.shape, bf16),
            pltpu.SMEM((shards,), jnp.int32),
            pltpu.VMEM((tokens, columns), bf16),
            pltpu.SemaphoreType.DMA((chunks,)),
            pltpu.SemaphoreType.DMA((chunks,)),
            pltpu.SemaphoreType.DMA((chunks,)),
            pltpu.SemaphoreType.DMA((4,)),
        ],
        compiler_params=pltpu.CompilerParams(vmem_limit_bytes=20 << 20),
        name="compress",
    )(base_step, *inputs)

    got = lax.all_to_all(send, "tok", split_axis=0, concat_axis=0, tiled=True)

    block_rows = query_count
    while block_rows * key_count * 4 > (4 << 20):
        block_rows //= 2
    attended = pl.pallas_call(
        functools.partial(attend_kernel, (per_dev, part_rows, rank, tokens, q_at, left_at), block_rows),
        out_shape=jax.ShapeDtypeStruct((query_count, LANES), bf16),
        in_specs=[vmem, vmem, vmem],
        out_specs=vmem,
        scratch_shapes=[
            pltpu.VMEM((per_dev, key_count, LANES), bf16),
            pltpu.VMEM((per_dev, key_count, LANES), bf16),
            pltpu.VMEM((per_dev, query_count, LANES), bf16),
        ],
        compiler_params=pltpu.CompilerParams(vmem_limit_bytes=32 << 20),
        name="attend",
    )(dead, got, cache)
    attended = attended.reshape(shards, part_rows, LANES)[:, :, :q_width]

    returned = lax.all_to_all(attended, "tok", split_axis=0, concat_axis=0, tiled=True)
    returned = returned.reshape(groups, parts, part_rows, q_width)
    row_block = returned.transpose(1, 2, 0, 3).reshape(query_rows, head_count * HD)
    chunks = 2
    return pl.pallas_call(
        project_kernel,
        out_shape=jax.ShapeDtypeStruct((query_rows, w_out.shape[1]), bf16),
        in_specs=[vmem, vmem],
        out_specs=hbm,
        scratch_shapes=[
            pltpu.VMEM((chunks, query_rows, w_out.shape[1] // chunks), bf16),
            pltpu.SemaphoreType.DMA((chunks,)),
        ],
        compiler_params=pltpu.CompilerParams(vmem_limit_bytes=8 << 20),
        name="project",
    )(row_block, w_out)


def solution(mesh):
    return jax.shard_map(
        per_device,
        mesh=mesh,
        in_specs=(
            P(("groups", "tok"), None),
            P(("groups", "tok"), None),
            P(None, ("groups", "tok"), None),
            P(("groups", "tok")),
            P("groups"),
            P(),
            P(("groups", "tok"), None, None),
            P(),
        ),
        out_specs=P(("groups", "tok"), None),
        check_vma=False,
    )
```

```python
import functools
import math

import jax
import jax.numpy as jnp
from jax import lax
from jax.experimental import pallas as pl
from jax.experimental.pallas import tpu as pltpu
from jax.sharding import PartitionSpec as P

HD = 64
SWEEPS = 2
LANES = 128
NT = (((1,), (1,)), ((), ()))
NN = (((1,), (0,)), ((), ()))
highest = lax.Precision.HIGHEST
f32 = jnp.float32
bf16 = jnp.bfloat16


def up(value, to):
    return -(-value // to) * to


def matmul(a, b, dims, precision=None):
    return lax.dot_general(a, b, dims, precision=precision, preferred_element_type=f32)


def split(x):
    high = x.astype(bf16)
    return high, (x - high.astype(f32)).astype(bf16)


def eliminate(m, cols):
    rank, wide = m.shape
    tile = 8
    rest = [m[i : i + tile] for i in range(0, rank, tile)]
    row_id = lax.broadcasted_iota(jnp.int32, (tile, wide), 0)
    spread = lambda x, i: jnp.broadcast_to(x[i : i + 1], (tile, wide))
    done = []
    for start in range(0, rank, tile):
        lane = [jnp.full((tile, wide), cols + start + k, jnp.int32) for k in range(tile)]
        col = [[jnp.take_along_axis(r, at, axis=1, mode="promise_in_bounds") for r in rest] for at in lane]
        row = [spread(rest[0], k) for k in range(tile)]
        head = jnp.zeros((tile, wide), f32)
        pivot = spread(col[0][0], 0)
        for k in range(tile):
            later = range(k + 1, tile)
            ahead = {a: spread(col[a][0], k) for a in later}
            following = spread(col[k + 1][0], k + 1) if k + 1 < tile else None
            root = lax.rsqrt(pivot)
            times = {a: ahead[a] * root for a in later}
            if k + 1 < tile:
                pivot = following - times[k + 1] * times[k + 1]
            row[k] = row[k] * root
            head = jnp.where(row_id == k, row[k], head)
            below = [c * root for c in col[k]]
            for a in later:
                row[a] = row[a] - times[a] * row[k]
                col[a] = [c - times[a] * d for c, d in zip(col[a], below)]
            for i in range(1, len(rest)):
                rest[i] = rest[i] - below[i] * row[k]
        done.append(head)
        rest = rest[1:]
    return jnp.concatenate(done, axis=0)


def compress_kernel(
    plan,
    base_ref,
    live_ref,
    new_ref,
    prev_ref,
    sketch_ref,
    q_ref,
    cache_ref,
    w_ref,
    out_ref,
    dead_ref,
    cache_out,
    w_out,
    new_buf,
    prev_buf,
    sketch_buf,
    q_buf,
    live_buf,
    terms,
    new_sems,
    prev_sems,
    sketch_sems,
    sems,
):
    tokens, columns = new_ref.shape
    rank = sketch_ref.shape[0]
    chunks = new_buf.shape[0]
    step = columns // chunks
    per_dev, parts, part_rows, q_at, left_at = plan
    receivers = out_ref.shape[0]
    groups = receivers // parts
    base = jnp.where(base_ref[0] == 1, 1, 0)
    q_copy = pltpu.make_async_copy(q_ref, q_buf, sems.at[0])
    live_copy = pltpu.make_async_copy(live_ref, live_buf, sems.at[1])
    live_copy.start()
    q_copy.start()
    copies = []
    for c in range(chunks):
        at = pl.ds(c * step, step)
        trio = (
            pltpu.make_async_copy(new_ref.at[:, at], new_buf.at[c], new_sems.at[c]),
            pltpu.make_async_copy(prev_ref.at[base, :, at], prev_buf.at[c], prev_sems.at[c]),
            pltpu.make_async_copy(sketch_ref.at[:, at], sketch_buf.at[c], sketch_sems.at[c]),
        )
        for copy in trio:
            copy.start()
        copies.append(trio)
    later = (
        pltpu.make_async_copy(cache_ref, cache_out, sems.at[2]),
        pltpu.make_async_copy(w_ref, w_out, sems.at[3]),
    )
    for copy in later:
        copy.start()

    live_copy.wait()
    row_t = lax.broadcasted_iota(jnp.int32, (tokens, LANES), 0)
    lane_t = lax.broadcasted_iota(jnp.int32, (tokens, LANES), 1)
    edge = jnp.where(lane_t == HD, row_t, -1)
    for s in range(receivers):
        dead_ref[s] = jnp.where(edge >= live_buf[s], -1e30, 0.0).astype(bf16)
    q_copy.wait()
    for g in range(groups):
        for j in range(parts):
            if q_buf.ndim == 2:
                block = q_buf[j * part_rows : (j + 1) * part_rows, g * LANES : (g + 1) * LANES]
            else:
                block = q_buf[g * parts + j]
            out_ref[g * parts + j, q_at : q_at + block.shape[0], :] = block * bf16(HD**-0.5)

    total = jnp.zeros((tokens + 2 * rank, tokens), f32)
    for c in range(chunks):
        at = slice(c * step, (c + 1) * step)
        for copy in copies[c]:
            copy.wait()
        high = (new_buf[c].astype(f32) - prev_buf[c].astype(f32)).astype(bf16)
        terms[:, at] = high
        s_high, s_low = split(sketch_buf[c])
        total = total + matmul(jnp.concatenate([high, s_high, s_low], axis=0), high, NT)
    gram = total[:tokens]
    y = total[tokens : tokens + rank] + total[tokens + rank :]

    eye = jnp.where(
        lax.broadcasted_iota(jnp.int32, (tokens, tokens), 0) == lax.broadcasted_iota(jnp.int32, (tokens, tokens), 1),
        1.0,
        0.0,
    )
    for sweep in range(SWEEPS + 1):
        if sweep:
            y = matmul(basis, gram, NN, highest)
        both = matmul(y, jnp.concatenate([eye, y], axis=0), NT, highest)
        basis = eliminate(both, tokens)[:, :tokens]

    high, low = split(basis)
    lhs = jnp.concatenate([high, low], axis=0)

    blocks = LANES // rank
    packed_rows = tokens // blocks
    tiled = jnp.concatenate([high] * blocks, axis=0)
    lane = lax.broadcasted_iota(jnp.int32, (packed_rows, LANES), 1)
    packed = jnp.zeros((packed_rows, LANES), f32)
    for k in range(blocks):
        pick = (
            lax.broadcasted_iota(jnp.int32, (packed_rows, tokens), 1)
            == lax.broadcasted_iota(jnp.int32, (packed_rows, tokens), 0) + k * packed_rows
        )
        packed = jnp.where(lane // rank == k, matmul(jnp.where(pick, 1.0, 0.0).astype(bf16), tiled, NT), packed)
    packed = packed.astype(bf16)

    width = 2 * HD * per_dev
    for g in range(groups):
        pair = matmul(lhs, terms[:, g * width : (g + 1) * width], NN)
        block = (pair[:rank] + pair[rank:]).astype(bf16)
        for j in range(parts):
            for d in range(per_dev):
                out_ref[g * parts + j, d * rank : (d + 1) * rank, :] = block[:, d * LANES : (d + 1) * LANES]
            out_ref[g * parts + j, left_at : left_at + packed_rows, :] = packed
    for copy in later:
        copy.wait()


def attend_kernel(plan, block_rows, dead_ref, got_ref, cache_ref, out_ref, keys, values, q_all):
    per_dev, part_rows, rank, tokens, q_at, left_at = plan
    shards = got_ref.shape[0]
    blocks = LANES // rank
    packed_rows = tokens // blocks
    lane_p = lax.broadcasted_iota(jnp.int32, (packed_rows, LANES), 1)
    is_key = lax.broadcasted_iota(jnp.int32, (tokens, LANES), 1) < HD
    ones = jnp.ones((tokens, LANES), bf16)

    def one_shard(s, carry):
        packed = got_ref[s, left_at : left_at + packed_rows, :].astype(f32)
        left = jnp.concatenate([jnp.where(lane_p // rank == k, packed, 0.0) for k in range(blocks)], axis=0).astype(bf16)
        at = pl.ds(pl.multiple_of(s * tokens, tokens), tokens)
        right = jnp.concatenate([got_ref[s, d * rank : (d + 1) * rank, :] for d in range(per_dev)], axis=1)
        lowrank = matmul(left, jnp.concatenate([right] * blocks, axis=0), NN).astype(bf16)
        for d in range(per_dev):
            both = cache_ref[d, at, :] + lowrank[:, d * LANES : (d + 1) * LANES]
            keys[d, at, :] = jnp.where(is_key, both, dead_ref[s])
            values[d, at, :] = jnp.where(is_key, ones, both)
        return carry

    lax.fori_loop(0, shards, one_shard, 0, unroll=math.gcd(shards, 16))

    padded = got_ref[:, q_at : q_at + up(part_rows, 16), :].astype(f32)
    q_rows = padded[:, :part_rows, :].reshape(shards * part_rows, LANES)
    lane_q = lax.broadcasted_iota(jnp.int32, q_rows.shape, 1)
    for d in range(per_dev):
        moved = q_rows if d == 0 else pltpu.roll(q_rows, LANES - d * HD, 1)
        q_all[d] = jnp.where(lane_q < HD, moved, jnp.where(lane_q == HD, 1.0, 0.0)).astype(bf16)

    part = block_rows // 2
    lane_o = lax.broadcasted_iota(jnp.int32, (part, LANES), 1)

    def one_block(b, carry):
        start = b * block_rows
        at = [pl.ds(start + i * part, part) for i in range(2)]
        out = [None] * 2
        for d in range(per_dev):
            scores = [matmul(q_all[d, at[i], :], keys[d], NT) for i in range(2)]
            exponent = [jnp.exp(x - jnp.max(x, axis=1, keepdims=True)).astype(bf16) for x in scores]
            for i in range(2):
                sums = matmul(exponent[i], values[d], NN)
                flipped = pltpu.roll(sums, HD, 1)
                if d == 0:
                    out[i] = flipped / sums
                else:
                    out[i] = jnp.where(lane_o < HD, out[i], sums / flipped)
        for i in range(2):
            out_ref[at[i], :] = out[i].astype(bf16)
        return carry

    count = shards * part_rows // block_rows
    if count == 1:
        one_block(0, 0)
    else:
        lax.fori_loop(0, count, one_block, 0)


def project_kernel(x_ref, w_ref, out_ref, buf, sems):
    chunks, rows, step = buf.shape
    copies = []
    for c in range(chunks):
        at = slice(c * step, (c + 1) * step)
        buf[c] = matmul(x_ref[...], w_ref[:, at], NN).astype(bf16)
        copies.append(pltpu.make_async_copy(buf.at[c], out_ref.at[:, pl.ds(c * step, step)], sems.at[c]))
        copies[c].start()
    for copy in copies:
        copy.wait()


def per_device(queries, new_kv, prev_kv, base_step, live_counts, sketch, cache, w_out):
    shards = lax.axis_size("tok")
    tokens, columns = new_kv.shape
    rank = sketch.shape[1]
    query_rows = queries.shape[0]
    head_count = queries.shape[1] // HD
    parts = max(1, shards // head_count)
    per_dev = head_count * parts // shards
    groups = head_count // per_dev
    part_rows = query_rows // parts
    key_count = shards * tokens
    query_count = shards * part_rows
    q_width = per_dev * HD

    q_at = per_dev * rank
    left_at = q_at + up(part_rows, 16)
    rows = left_at + tokens * rank // LANES
    if q_width == LANES and part_rows % 16 == 0:
        q_in = queries
    else:
        q_in = queries.reshape(parts, part_rows, groups, q_width).transpose(2, 0, 1, 3)
        q_in = q_in.reshape(shards, part_rows, q_width)
        q_in = jnp.pad(q_in, ((0, 0), (0, up(part_rows, 16) - part_rows), (0, LANES - q_width)))

    vmem = pl.BlockSpec(memory_space=pltpu.VMEM)
    smem = pl.BlockSpec(memory_space=pltpu.SMEM)
    chunks = 4
    step = columns // chunks
    hbm = pl.BlockSpec(memory_space=pltpu.HBM)
    inputs = (live_counts, new_kv, prev_kv, sketch.T, q_in, cache, w_out)
    inputs = [pltpu.with_memory_space_constraint(x, pltpu.HBM) for x in inputs]
    send, dead, cache, w_out = pl.pallas_call(
        functools.partial(compress_kernel, (per_dev, parts, part_rows, q_at, left_at)),
        out_shape=(
            jax.ShapeDtypeStruct((shards, rows, LANES), bf16),
            jax.ShapeDtypeStruct((shards, tokens, LANES), bf16),
            jax.ShapeDtypeStruct(cache.shape, bf16),
            jax.ShapeDtypeStruct(w_out.shape, bf16),
        ),
        in_specs=[smem] + [hbm] * 7,
        out_specs=(vmem,) * 4,
        scratch_shapes=[
            pltpu.VMEM((chunks, tokens, step), bf16),
            pltpu.VMEM((chunks, tokens, step), bf16),
            pltpu.VMEM((chunks, rank, step), f32),
            pltpu.VMEM(q_in.shape, bf16),
            pltpu.SMEM((shards,), jnp.int32),
            pltpu.VMEM((tokens, columns), bf16),
            pltpu.SemaphoreType.DMA((chunks,)),
            pltpu.SemaphoreType.DMA((chunks,)),
            pltpu.SemaphoreType.DMA((chunks,)),
            pltpu.SemaphoreType.DMA((4,)),
        ],
        compiler_params=pltpu.CompilerParams(vmem_limit_bytes=20 << 20),
        name="compress",
    )(base_step, *inputs)

    got = lax.all_to_all(send, "tok", split_axis=0, concat_axis=0, tiled=True)

    block_rows = query_count
    while block_rows * key_count * 4 > (4 << 20):
        block_rows //= 2
    attended = pl.pallas_call(
        functools.partial(attend_kernel, (per_dev, part_rows, rank, tokens, q_at, left_at), block_rows),
        out_shape=jax.ShapeDtypeStruct((query_count, LANES), bf16),
        in_specs=[vmem, vmem, vmem],
        out_specs=vmem,
        scratch_shapes=[
            pltpu.VMEM((per_dev, key_count, LANES), bf16),
            pltpu.VMEM((per_dev, key_count, LANES), bf16),
            pltpu.VMEM((per_dev, query_count, LANES), bf16),
        ],
        compiler_params=pltpu.CompilerParams(vmem_limit_bytes=32 << 20),
        name="attend",
    )(dead, got, cache)
    attended = attended.reshape(shards, part_rows, LANES)[:, :, :q_width]

    returned = lax.all_to_all(attended, "tok", split_axis=0, concat_axis=0, tiled=True)
    returned = returned.reshape(groups, parts, part_rows, q_width)
    row_block = returned.transpose(1, 2, 0, 3).reshape(query_rows, head_count * HD)
    chunks = 2
    return pl.pallas_call(
        project_kernel,
        out_shape=jax.ShapeDtypeStruct((query_rows, w_out.shape[1]), bf16),
        in_specs=[vmem, vmem],
        out_specs=hbm,
        scratch_shapes=[
            pltpu.VMEM((chunks, query_rows, w_out.shape[1] // chunks), bf16),
            pltpu.SemaphoreType.DMA((chunks,)),
        ],
        compiler_params=pltpu.CompilerParams(vmem_limit_bytes=8 << 20),
        name="project",
    )(row_block, w_out)


def solution(mesh):
    return jax.shard_map(
        per_device,
        mesh=mesh,
        in_specs=(
            P(("groups", "tok"), None),
            P(("groups", "tok"), None),
            P(None, ("groups", "tok"), None),
            P(("groups", "tok")),
            P("groups"),
            P(),
            P(("groups", "tok"), None, None),
            P(),
        ),
        out_specs=P(("groups", "tok"), None),
        check_vma=False,
    )
```

```python
import functools
import math

import jax
import jax.numpy as jnp
from jax import lax
from jax.experimental import pallas as pl
from jax.experimental.pallas import tpu as pltpu
from jax.sharding import PartitionSpec as P

HD = 64
SWEEPS = 2
LANES = 128
NT = (((1,), (1,)), ((), ()))
NN = (((1,), (0,)), ((), ()))
highest = lax.Precision.HIGHEST
f32 = jnp.float32
bf16 = jnp.bfloat16


def up(value, to):
    return -(-value // to) * to


def matmul(a, b, dims, precision=None):
    return lax.dot_general(a, b, dims, precision=precision, preferred_element_type=f32)


def split(x):
    high = x.astype(bf16)
    return high, (x - high.astype(f32)).astype(bf16)


def eliminate(m, cols):
    rank, wide = m.shape
    tile = 8
    rest = [m[i : i + tile] for i in range(0, rank, tile)]
    row_id = lax.broadcasted_iota(jnp.int32, (tile, wide), 0)
    spread = lambda x, i: jnp.broadcast_to(x[i : i + 1], (tile, wide))
    done = []
    for start in range(0, rank, tile):
        lane = [jnp.full((tile, wide), cols + start + k, jnp.int32) for k in range(tile)]
        col = [[jnp.take_along_axis(r, at, axis=1, mode="promise_in_bounds") for r in rest] for at in lane]
        row = [spread(rest[0], k) for k in range(tile)]
        head = jnp.zeros((tile, wide), f32)
        pivot = spread(col[0][0], 0)
        for k in range(tile):
            later = range(k + 1, tile)
            ahead = {a: spread(col[a][0], k) for a in later}
            following = spread(col[k + 1][0], k + 1) if k + 1 < tile else None
            root = lax.rsqrt(pivot)
            times = {a: ahead[a] * root for a in later}
            if k + 1 < tile:
                pivot = following - times[k + 1] * times[k + 1]
            row[k] = row[k] * root
            head = jnp.where(row_id == k, row[k], head)
            below = [c * root for c in col[k]]
            for a in later:
                row[a] = row[a] - times[a] * row[k]
                col[a] = [c - times[a] * d for c, d in zip(col[a], below)]
            for i in range(1, len(rest)):
                rest[i] = rest[i] - below[i] * row[k]
        done.append(head)
        rest = rest[1:]
    return jnp.concatenate(done, axis=0)


def compress_kernel(
    plan,
    base_ref,
    live_ref,
    new_ref,
    prev_ref,
    sketch_ref,
    q_ref,
    cache_ref,
    w_ref,
    out_ref,
    dead_ref,
    cache_out,
    w_out,
    new_buf,
    prev_buf,
    sketch_buf,
    q_buf,
    live_buf,
    terms,
    new_sems,
    prev_sems,
    sketch_sems,
    sems,
):
    tokens, columns = new_ref.shape
    rank = sketch_ref.shape[0]
    chunks = new_buf.shape[0]
    step = columns // chunks
    per_dev, parts, part_rows, q_at, left_at = plan
    receivers = out_ref.shape[0]
    groups = receivers // parts
    base = jnp.where(base_ref[0] == 1, 1, 0)
    q_copy = pltpu.make_async_copy(q_ref, q_buf, sems.at[0])
    live_copy = pltpu.make_async_copy(live_ref, live_buf, sems.at[1])
    live_copy.start()
    q_copy.start()
    copies = []
    for c in range(chunks):
        at = pl.ds(c * step, step)
        trio = (
            pltpu.make_async_copy(new_ref.at[:, at], new_buf.at[c], new_sems.at[c]),
            pltpu.make_async_copy(prev_ref.at[base, :, at], prev_buf.at[c], prev_sems.at[c]),
            pltpu.make_async_copy(sketch_ref.at[:, at], sketch_buf.at[c], sketch_sems.at[c]),
        )
        for copy in trio:
            copy.start()
        copies.append(trio)
    later = (
        pltpu.make_async_copy(cache_ref, cache_out, sems.at[2]),
        pltpu.make_async_copy(w_ref, w_out, sems.at[3]),
    )
    for copy in later:
        copy.start()

    live_copy.wait()
    row_t = lax.broadcasted_iota(jnp.int32, (tokens, LANES), 0)
    lane_t = lax.broadcasted_iota(jnp.int32, (tokens, LANES), 1)
    edge = jnp.where(lane_t == HD, row_t, -1)
    for s in range(receivers):
        dead_ref[s] = jnp.where(edge >= live_buf[s], -1e30, 0.0).astype(bf16)
    q_copy.wait()
    for g in range(groups):
        for j in range(parts):
            if q_buf.ndim == 2:
                block = q_buf[j * part_rows : (j + 1) * part_rows, g * LANES : (g + 1) * LANES]
            else:
                block = q_buf[g * parts + j]
            out_ref[g * parts + j, q_at : q_at + block.shape[0], :] = block * bf16(HD**-0.5)

    total = jnp.zeros((tokens + 2 * rank, tokens), f32)
    for c in range(chunks):
        at = slice(c * step, (c + 1) * step)
        for copy in copies[c]:
            copy.wait()
        high = (new_buf[c].astype(f32) - prev_buf[c].astype(f32)).astype(bf16)
        terms[:, at] = high
        s_high, s_low = split(sketch_buf[c])
        total = total + matmul(jnp.concatenate([high, s_high, s_low], axis=0), high, NT)
    gram = total[:tokens]
    y = total[tokens : tokens + rank] + total[tokens + rank :]

    eye = jnp.where(
        lax.broadcasted_iota(jnp.int32, (tokens, tokens), 0) == lax.broadcasted_iota(jnp.int32, (tokens, tokens), 1),
        1.0,
        0.0,
    )
    for sweep in range(SWEEPS + 1):
        if sweep:
            y = matmul(basis, gram, NN, highest)
        both = matmul(y, jnp.concatenate([eye, y], axis=0), NT, highest)
        basis = eliminate(both, tokens)[:, :tokens]

    high, low = split(basis)
    lhs = jnp.concatenate([high, low], axis=0)

    blocks = LANES // rank
    packed_rows = tokens // blocks
    tiled = jnp.concatenate([high] * blocks, axis=0)
    lane = lax.broadcasted_iota(jnp.int32, (packed_rows, LANES), 1)
    packed = jnp.zeros((packed_rows, LANES), f32)
    for k in range(blocks):
        pick = (
            lax.broadcasted_iota(jnp.int32, (packed_rows, tokens), 1)
            == lax.broadcasted_iota(jnp.int32, (packed_rows, tokens), 0) + k * packed_rows
        )
        packed = jnp.where(lane // rank == k, matmul(jnp.where(pick, 1.0, 0.0).astype(bf16), tiled, NT), packed)
    packed = packed.astype(bf16)

    width = 2 * HD * per_dev
    for g in range(groups):
        pair = matmul(lhs, terms[:, g * width : (g + 1) * width], NN)
        block = (pair[:rank] + pair[rank:]).astype(bf16)
        for j in range(parts):
            for d in range(per_dev):
                out_ref[g * parts + j, d * rank : (d + 1) * rank, :] = block[:, d * LANES : (d + 1) * LANES]
            out_ref[g * parts + j, left_at : left_at + packed_rows, :] = packed
    for copy in later:
        copy.wait()


def attend_kernel(plan, block_rows, dead_ref, got_ref, cache_ref, out_ref, keys, values, q_all):
    per_dev, part_rows, rank, tokens, q_at, left_at = plan
    shards = got_ref.shape[0]
    blocks = LANES // rank
    packed_rows = tokens // blocks
    lane_p = lax.broadcasted_iota(jnp.int32, (packed_rows, LANES), 1)
    is_key = lax.broadcasted_iota(jnp.int32, (tokens, LANES), 1) < HD
    ones = jnp.ones((tokens, LANES), bf16)

    def one_shard(s, carry):
        packed = got_ref[s, left_at : left_at + packed_rows, :].astype(f32)
        left = jnp.concatenate([jnp.where(lane_p // rank == k, packed, 0.0) for k in range(blocks)], axis=0).astype(bf16)
        at = pl.ds(pl.multiple_of(s * tokens, tokens), tokens)
        right = jnp.concatenate([got_ref[s, d * rank : (d + 1) * rank, :] for d in range(per_dev)], axis=1)
        lowrank = matmul(left, jnp.concatenate([right] * blocks, axis=0), NN).astype(bf16)
        for d in range(per_dev):
            both = cache_ref[d, at, :] + lowrank[:, d * LANES : (d + 1) * LANES]
            keys[d, at, :] = jnp.where(is_key, both, dead_ref[s])
            values[d, at, :] = jnp.where(is_key, ones, both)
        return carry

    lax.fori_loop(0, shards, one_shard, 0, unroll=math.gcd(shards, 16))

    padded = got_ref[:, q_at : q_at + up(part_rows, 16), :].astype(f32)
    q_rows = padded[:, :part_rows, :].reshape(shards * part_rows, LANES)
    lane_q = lax.broadcasted_iota(jnp.int32, q_rows.shape, 1)
    for d in range(per_dev):
        moved = q_rows if d == 0 else pltpu.roll(q_rows, LANES - d * HD, 1)
        q_all[d] = jnp.where(lane_q < HD, moved, jnp.where(lane_q == HD, 1.0, 0.0)).astype(bf16)

    part = block_rows // 2
    lane_o = lax.broadcasted_iota(jnp.int32, (part, LANES), 1)

    def one_block(b, carry):
        start = b * block_rows
        at = [pl.ds(start + i * part, part) for i in range(2)]
        out = [None] * 2
        for d in range(per_dev):
            scores = [matmul(q_all[d, at[i], :], keys[d], NT) for i in range(2)]
            exponent = [jnp.exp(x - jnp.max(x, axis=1, keepdims=True)).astype(bf16) for x in scores]
            for i in range(2):
                sums = matmul(exponent[i], values[d], NN)
                flipped = pltpu.roll(sums, HD, 1)
                if d == 0:
                    out[i] = flipped / sums
                else:
                    out[i] = jnp.where(lane_o < HD, out[i], sums / flipped)
        for i in range(2):
            out_ref[at[i], :] = out[i].astype(bf16)
        return carry

    count = shards * part_rows // block_rows
    if count == 1:
        one_block(0, 0)
    else:
        lax.fori_loop(0, count, one_block, 0)


def project_kernel(x_ref, w_ref, out_ref, buf, sems):
    chunks, rows, step = buf.shape
    if x_ref.ndim == 3:
        x = jnp.concatenate([x_ref[i] for i in range(x_ref.shape[0])], axis=1)
    else:
        x = x_ref[...]
    copies = []
    for c in range(chunks):
        at = slice(c * step, (c + 1) * step)
        buf[c] = matmul(x, w_ref[:, at], NN).astype(bf16)
        copies.append(pltpu.make_async_copy(buf.at[c], out_ref.at[:, pl.ds(c * step, step)], sems.at[c]))
        copies[c].start()
    for copy in copies:
        copy.wait()


def per_device(queries, new_kv, prev_kv, base_step, live_counts, sketch, cache, w_out):
    shards = lax.axis_size("tok")
    tokens, columns = new_kv.shape
    rank = sketch.shape[1]
    query_rows = queries.shape[0]
    head_count = queries.shape[1] // HD
    parts = max(1, shards // head_count)
    per_dev = head_count * parts // shards
    groups = head_count // per_dev
    part_rows = query_rows // parts
    key_count = shards * tokens
    query_count = shards * part_rows
    q_width = per_dev * HD

    q_at = per_dev * rank
    left_at = q_at + up(part_rows, 16)
    rows = left_at + tokens * rank // LANES
    if q_width == LANES and part_rows % 16 == 0:
        q_in = queries
    else:
        q_in = queries.reshape(parts, part_rows, groups, q_width).transpose(2, 0, 1, 3)
        q_in = q_in.reshape(shards, part_rows, q_width)
        q_in = jnp.pad(q_in, ((0, 0), (0, up(part_rows, 16) - part_rows), (0, LANES - q_width)))

    vmem = pl.BlockSpec(memory_space=pltpu.VMEM)
    smem = pl.BlockSpec(memory_space=pltpu.SMEM)
    chunks = 4
    step = columns // chunks
    hbm = pl.BlockSpec(memory_space=pltpu.HBM)
    inputs = (live_counts, new_kv, prev_kv, sketch.T, q_in, cache, w_out)
    inputs = [pltpu.with_memory_space_constraint(x, pltpu.HBM) for x in inputs]
    send, dead, cache, w_out = pl.pallas_call(
        functools.partial(compress_kernel, (per_dev, parts, part_rows, q_at, left_at)),
        out_shape=(
            jax.ShapeDtypeStruct((shards, rows, LANES), bf16),
            jax.ShapeDtypeStruct((shards, tokens, LANES), bf16),
            jax.ShapeDtypeStruct(cache.shape, bf16),
            jax.ShapeDtypeStruct(w_out.shape, bf16),
        ),
        in_specs=[smem] + [hbm] * 7,
        out_specs=(vmem,) * 4,
        scratch_shapes=[
            pltpu.VMEM((chunks, tokens, step), bf16),
            pltpu.VMEM((chunks, tokens, step), bf16),
            pltpu.VMEM((chunks, rank, step), f32),
            pltpu.VMEM(q_in.shape, bf16),
            pltpu.SMEM((shards,), jnp.int32),
            pltpu.VMEM((tokens, columns), bf16),
            pltpu.SemaphoreType.DMA((chunks,)),
            pltpu.SemaphoreType.DMA((chunks,)),
            pltpu.SemaphoreType.DMA((chunks,)),
            pltpu.SemaphoreType.DMA((4,)),
        ],
        compiler_params=pltpu.CompilerParams(vmem_limit_bytes=20 << 20),
        name="compress",
    )(base_step, *inputs)

    got = lax.all_to_all(send, "tok", split_axis=0, concat_axis=0, tiled=True)

    block_rows = query_count
    while block_rows * key_count * 4 > (4 << 20):
        block_rows //= 2
    attended = pl.pallas_call(
        functools.partial(attend_kernel, (per_dev, part_rows, rank, tokens, q_at, left_at), block_rows),
        out_shape=jax.ShapeDtypeStruct((query_count, LANES), bf16),
        in_specs=[vmem, vmem, vmem],
        out_specs=vmem,
        scratch_shapes=[
            pltpu.VMEM((per_dev, key_count, LANES), bf16),
            pltpu.VMEM((per_dev, key_count, LANES), bf16),
            pltpu.VMEM((per_dev, query_count, LANES), bf16),
        ],
        compiler_params=pltpu.CompilerParams(vmem_limit_bytes=32 << 20),
        name="attend",
    )(dead, got, cache)
    attended = attended.reshape(shards, part_rows, LANES)[:, :, :q_width]

    returned = lax.all_to_all(attended, "tok", split_axis=0, concat_axis=0, tiled=True)
    if parts == 1 and q_width == LANES:
        row_block = returned
    else:
        returned = returned.reshape(groups, parts, part_rows, q_width)
        row_block = returned.transpose(1, 2, 0, 3).reshape(query_rows, head_count * HD)
    chunks = 2
    return pl.pallas_call(
        project_kernel,
        out_shape=jax.ShapeDtypeStruct((query_rows, w_out.shape[1]), bf16),
        in_specs=[vmem, vmem],
        out_specs=hbm,
        scratch_shapes=[
            pltpu.VMEM((chunks, query_rows, w_out.shape[1] // chunks), bf16),
            pltpu.SemaphoreType.DMA((chunks,)),
        ],
        compiler_params=pltpu.CompilerParams(vmem_limit_bytes=8 << 20),
        name="project",
    )(row_block, w_out)


def solution(mesh):
    return jax.shard_map(
        per_device,
        mesh=mesh,
        in_specs=(
            P(("groups", "tok"), None),
            P(("groups", "tok"), None),
            P(None, ("groups", "tok"), None),
            P(("groups", "tok")),
            P("groups"),
            P(),
            P(("groups", "tok"), None, None),
            P(),
        ),
        out_specs=P(("groups", "tok"), None),
        check_vma=False,
    )
```

```python
import functools
import math

import jax
import jax.numpy as jnp
from jax import lax
from jax.experimental import pallas as pl
from jax.experimental.pallas import tpu as pltpu
from jax.sharding import PartitionSpec as P

HD = 64
SWEEPS = 2
LANES = 128
NT = (((1,), (1,)), ((), ()))
NN = (((1,), (0,)), ((), ()))
highest = lax.Precision.HIGHEST
f32 = jnp.float32
bf16 = jnp.bfloat16


def up(value, to):
    return -(-value // to) * to


def matmul(a, b, dims, precision=None):
    return lax.dot_general(a, b, dims, precision=precision, preferred_element_type=f32)


def split(x):
    high = x.astype(bf16)
    return high, (x - high.astype(f32)).astype(bf16)


def eliminate(m, cols):
    rank, wide = m.shape
    tile = 8
    rest = [m[i : i + tile] for i in range(0, rank, tile)]
    row_id = lax.broadcasted_iota(jnp.int32, (tile, wide), 0)
    spread = lambda x, i: jnp.broadcast_to(x[i : i + 1], (tile, wide))
    done = []
    for start in range(0, rank, tile):
        lane = [jnp.full((tile, wide), cols + start + k, jnp.int32) for k in range(tile)]
        col = [[jnp.take_along_axis(r, at, axis=1, mode="promise_in_bounds") for r in rest] for at in lane]
        row = [spread(rest[0], k) for k in range(tile)]
        head = jnp.zeros((tile, wide), f32)
        pivot = spread(col[0][0], 0)
        for k in range(tile):
            later = range(k + 1, tile)
            ahead = {a: spread(col[a][0], k) for a in later}
            following = spread(col[k + 1][0], k + 1) if k + 1 < tile else None
            root = lax.rsqrt(pivot)
            times = {a: ahead[a] * root for a in later}
            if k + 1 < tile:
                pivot = following - times[k + 1] * times[k + 1]
            row[k] = row[k] * root
            head = jnp.where(row_id == k, row[k], head)
            below = [c * root for c in col[k]]
            for a in later:
                row[a] = row[a] - times[a] * row[k]
                col[a] = [c - times[a] * d for c, d in zip(col[a], below)]
            for i in range(1, len(rest)):
                rest[i] = rest[i] - below[i] * row[k]
        done.append(head)
        rest = rest[1:]
    return jnp.concatenate(done, axis=0)


def compress_kernel(
    plan,
    base_ref,
    live_ref,
    new_ref,
    prev_ref,
    sketch_ref,
    q_ref,
    cache_ref,
    w_ref,
    out_ref,
    dead_ref,
    cache_out,
    w_out,
    new_buf,
    prev_buf,
    sketch_buf,
    q_buf,
    live_buf,
    terms,
    new_sems,
    prev_sems,
    sketch_sems,
    sems,
):
    tokens, columns = new_ref.shape
    rank = sketch_ref.shape[0]
    chunks = new_buf.shape[0]
    step = columns // chunks
    per_dev, parts, part_rows, q_at, left_at = plan
    receivers = out_ref.shape[0]
    groups = receivers // parts
    base = jnp.where(base_ref[0] == 1, 1, 0)
    q_copy = pltpu.make_async_copy(q_ref, q_buf, sems.at[0])
    live_copy = pltpu.make_async_copy(live_ref, live_buf, sems.at[1])
    live_copy.start()
    q_copy.start()
    copies = []
    for c in range(chunks):
        at = pl.ds(c * step, step)
        trio = (
            pltpu.make_async_copy(new_ref.at[:, at], new_buf.at[c], new_sems.at[c]),
            pltpu.make_async_copy(prev_ref.at[base, :, at], prev_buf.at[c], prev_sems.at[c]),
            pltpu.make_async_copy(sketch_ref.at[:, at], sketch_buf.at[c], sketch_sems.at[c]),
        )
        for copy in trio:
            copy.start()
        copies.append(trio)
    later = (
        pltpu.make_async_copy(cache_ref, cache_out, sems.at[2]),
        pltpu.make_async_copy(w_ref, w_out, sems.at[3]),
    )
    for copy in later:
        copy.start()

    live_copy.wait()
    row_t = lax.broadcasted_iota(jnp.int32, (tokens, LANES), 0)
    lane_t = lax.broadcasted_iota(jnp.int32, (tokens, LANES), 1)
    edge = jnp.where(lane_t == HD, row_t, -1)
    for s in range(receivers):
        dead_ref[s] = jnp.where(edge >= live_buf[s], -1e30, 0.0).astype(bf16)
    q_copy.wait()
    for g in range(groups):
        for j in range(parts):
            if q_buf.ndim == 2:
                block = q_buf[j * part_rows : (j + 1) * part_rows, g * LANES : (g + 1) * LANES]
            else:
                block = q_buf[g * parts + j]
            out_ref[g * parts + j, q_at : q_at + block.shape[0], :] = block * bf16(HD**-0.5)

    total = jnp.zeros((tokens + 2 * rank, tokens), f32)
    for c in range(chunks):
        at = slice(c * step, (c + 1) * step)
        for copy in copies[c]:
            copy.wait()
        high = (new_buf[c].astype(f32) - prev_buf[c].astype(f32)).astype(bf16)
        terms[:, at] = high
        s_high, s_low = split(sketch_buf[c])
        total = total + matmul(jnp.concatenate([high, s_high, s_low], axis=0), high, NT)
    gram = total[:tokens]
    y = total[tokens : tokens + rank] + total[tokens + rank :]

    eye = jnp.where(
        lax.broadcasted_iota(jnp.int32, (tokens, tokens), 0) == lax.broadcasted_iota(jnp.int32, (tokens, tokens), 1),
        1.0,
        0.0,
    )
    for sweep in range(SWEEPS + 1):
        if sweep:
            y = matmul(basis, gram, NN, highest)
        both = matmul(y, jnp.concatenate([eye, y], axis=0), NT, highest)
        basis = eliminate(both, tokens)[:, :tokens]

    high, low = split(basis)
    lhs = jnp.concatenate([high, low], axis=0)

    blocks = LANES // rank
    packed_rows = tokens // blocks
    tiled = jnp.concatenate([high] * blocks, axis=0)
    lane = lax.broadcasted_iota(jnp.int32, (packed_rows, LANES), 1)
    packed = jnp.zeros((packed_rows, LANES), f32)
    for k in range(blocks):
        pick = (
            lax.broadcasted_iota(jnp.int32, (packed_rows, tokens), 1)
            == lax.broadcasted_iota(jnp.int32, (packed_rows, tokens), 0) + k * packed_rows
        )
        packed = jnp.where(lane // rank == k, matmul(jnp.where(pick, 1.0, 0.0).astype(bf16), tiled, NT), packed)
    packed = packed.astype(bf16)

    width = 2 * HD * per_dev
    for g in range(groups):
        pair = matmul(lhs, terms[:, g * width : (g + 1) * width], NN)
        block = (pair[:rank] + pair[rank:]).astype(bf16)
        for j in range(parts):
            for d in range(per_dev):
                out_ref[g * parts + j, d * rank : (d + 1) * rank, :] = block[:, d * LANES : (d + 1) * LANES]
            out_ref[g * parts + j, left_at : left_at + packed_rows, :] = packed
    for copy in later:
        copy.wait()


def attend_kernel(plan, block_rows, dead_ref, got_ref, cache_ref, out_ref, keys, values, q_all):
    per_dev, part_rows, rank, tokens, q_at, left_at = plan
    shards = got_ref.shape[0]
    blocks = LANES // rank
    packed_rows = tokens // blocks
    lane_p = lax.broadcasted_iota(jnp.int32, (packed_rows, LANES), 1)
    is_key = lax.broadcasted_iota(jnp.int32, (tokens, LANES), 1) < HD
    ones = jnp.ones((tokens, LANES), bf16)

    def one_shard(s, carry):
        packed = got_ref[s, left_at : left_at + packed_rows, :].astype(f32)
        left = jnp.concatenate([jnp.where(lane_p // rank == k, packed, 0.0) for k in range(blocks)], axis=0).astype(bf16)
        at = pl.ds(pl.multiple_of(s * tokens, tokens), tokens)
        right = jnp.concatenate([got_ref[s, d * rank : (d + 1) * rank, :] for d in range(per_dev)], axis=1)
        lowrank = matmul(left, jnp.concatenate([right] * blocks, axis=0), NN).astype(bf16)
        for d in range(per_dev):
            both = cache_ref[d, at, :] + lowrank[:, d * LANES : (d + 1) * LANES]
            keys[d, at, :] = jnp.where(is_key, both, dead_ref[s])
            values[d, at, :] = jnp.where(is_key, ones, both)
        return carry

    lax.fori_loop(0, shards, one_shard, 0, unroll=math.gcd(shards, 16))

    padded = got_ref[:, q_at : q_at + up(part_rows, 16), :].astype(f32)
    q_rows = padded[:, :part_rows, :].reshape(shards * part_rows, LANES)
    lane_q = lax.broadcasted_iota(jnp.int32, q_rows.shape, 1)
    for d in range(per_dev):
        moved = q_rows if d == 0 else pltpu.roll(q_rows, LANES - d * HD, 1)
        q_all[d] = jnp.where(lane_q < HD, moved, jnp.where(lane_q == HD, 1.0, 0.0)).astype(bf16)

    part = block_rows // 2
    lane_o = lax.broadcasted_iota(jnp.int32, (part, LANES), 1)

    def one_block(b, carry):
        start = b * block_rows
        at = [pl.ds(start + i * part, part) for i in range(2)]
        out = [None] * 2
        all_scores = [[matmul(q_all[d, at[i], :], keys[d], NT) for i in range(2)] for d in range(per_dev)]
        for d in range(per_dev):
            scores = all_scores[d]
            exponent = [jnp.exp(x - jnp.max(x, axis=1, keepdims=True)).astype(bf16) for x in scores]
            for i in range(2):
                sums = matmul(exponent[i], values[d], NN)
                flipped = pltpu.roll(sums, HD, 1)
                if d == 0:
                    out[i] = flipped / sums
                else:
                    out[i] = jnp.where(lane_o < HD, out[i], sums / flipped)
        for i in range(2):
            out_ref[at[i], :] = out[i].astype(bf16)
        return carry

    count = shards * part_rows // block_rows
    if count == 1:
        one_block(0, 0)
    else:
        lax.fori_loop(0, count, one_block, 0)


def project_kernel(x_ref, w_ref, out_ref, buf, sems):
    chunks, rows, step = buf.shape
    if x_ref.ndim == 3:
        x = jnp.concatenate([x_ref[i] for i in range(x_ref.shape[0])], axis=1)
    else:
        x = x_ref[...]
    copies = []
    for c in range(chunks):
        at = slice(c * step, (c + 1) * step)
        buf[c] = matmul(x, w_ref[:, at], NN).astype(bf16)
        copies.append(pltpu.make_async_copy(buf.at[c], out_ref.at[:, pl.ds(c * step, step)], sems.at[c]))
        copies[c].start()
    for copy in copies:
        copy.wait()


def per_device(queries, new_kv, prev_kv, base_step, live_counts, sketch, cache, w_out):
    shards = lax.axis_size("tok")
    tokens, columns = new_kv.shape
    rank = sketch.shape[1]
    query_rows = queries.shape[0]
    head_count = queries.shape[1] // HD
    parts = max(1, shards // head_count)
    per_dev = head_count * parts // shards
    groups = head_count // per_dev
    part_rows = query_rows // parts
    key_count = shards * tokens
    query_count = shards * part_rows
    q_width = per_dev * HD

    q_at = per_dev * rank
    left_at = q_at + up(part_rows, 16)
    rows = left_at + tokens * rank // LANES
    if q_width == LANES and part_rows % 16 == 0:
        q_in = queries
    else:
        q_in = queries.reshape(parts, part_rows, groups, q_width).transpose(2, 0, 1, 3)
        q_in = q_in.reshape(shards, part_rows, q_width)
        q_in = jnp.pad(q_in, ((0, 0), (0, up(part_rows, 16) - part_rows), (0, LANES - q_width)))

    vmem = pl.BlockSpec(memory_space=pltpu.VMEM)
    smem = pl.BlockSpec(memory_space=pltpu.SMEM)
    chunks = 4
    step = columns // chunks
    hbm = pl.BlockSpec(memory_space=pltpu.HBM)
    inputs = (live_counts, new_kv, prev_kv, sketch.T, q_in, cache, w_out)
    inputs = [pltpu.with_memory_space_constraint(x, pltpu.HBM) for x in inputs]
    send, dead, cache, w_out = pl.pallas_call(
        functools.partial(compress_kernel, (per_dev, parts, part_rows, q_at, left_at)),
        out_shape=(
            jax.ShapeDtypeStruct((shards, rows, LANES), bf16),
            jax.ShapeDtypeStruct((shards, tokens, LANES), bf16),
            jax.ShapeDtypeStruct(cache.shape, bf16),
            jax.ShapeDtypeStruct(w_out.shape, bf16),
        ),
        in_specs=[smem] + [hbm] * 7,
        out_specs=(vmem,) * 4,
        scratch_shapes=[
            pltpu.VMEM((chunks, tokens, step), bf16),
            pltpu.VMEM((chunks, tokens, step), bf16),
            pltpu.VMEM((chunks, rank, step), f32),
            pltpu.VMEM(q_in.shape, bf16),
            pltpu.SMEM((shards,), jnp.int32),
            pltpu.VMEM((tokens, columns), bf16),
            pltpu.SemaphoreType.DMA((chunks,)),
            pltpu.SemaphoreType.DMA((chunks,)),
            pltpu.SemaphoreType.DMA((chunks,)),
            pltpu.SemaphoreType.DMA((4,)),
        ],
        compiler_params=pltpu.CompilerParams(vmem_limit_bytes=20 << 20),
        name="compress",
    )(base_step, *inputs)

    got = lax.all_to_all(send, "tok", split_axis=0, concat_axis=0, tiled=True)

    block_rows = query_count
    while block_rows * key_count * 4 > (4 << 20):
        block_rows //= 2
    attended = pl.pallas_call(
        functools.partial(attend_kernel, (per_dev, part_rows, rank, tokens, q_at, left_at), block_rows),
        out_shape=jax.ShapeDtypeStruct((query_count, LANES), bf16),
        in_specs=[vmem, vmem, vmem],
        out_specs=vmem,
        scratch_shapes=[
            pltpu.VMEM((per_dev, key_count, LANES), bf16),
            pltpu.VMEM((per_dev, key_count, LANES), bf16),
            pltpu.VMEM((per_dev, query_count, LANES), bf16),
        ],
        compiler_params=pltpu.CompilerParams(vmem_limit_bytes=32 << 20),
        name="attend",
    )(dead, got, cache)
    attended = attended.reshape(shards, part_rows, LANES)[:, :, :q_width]

    returned = lax.all_to_all(attended, "tok", split_axis=0, concat_axis=0, tiled=True)
    if parts == 1 and q_width == LANES:
        row_block = returned
    else:
        returned = returned.reshape(groups, parts, part_rows, q_width)
        row_block = returned.transpose(1, 2, 0, 3).reshape(query_rows, head_count * HD)
    chunks = 2
    return pl.pallas_call(
        project_kernel,
        out_shape=jax.ShapeDtypeStruct((query_rows, w_out.shape[1]), bf16),
        in_specs=[vmem, vmem],
        out_specs=hbm,
        scratch_shapes=[
            pltpu.VMEM((chunks, query_rows, w_out.shape[1] // chunks), bf16),
            pltpu.SemaphoreType.DMA((chunks,)),
        ],
        compiler_params=pltpu.CompilerParams(vmem_limit_bytes=8 << 20),
        name="project",
    )(row_block, w_out)


def solution(mesh):
    return jax.shard_map(
        per_device,
        mesh=mesh,
        in_specs=(
            P(("groups", "tok"), None),
            P(("groups", "tok"), None),
            P(None, ("groups", "tok"), None),
            P(("groups", "tok")),
            P("groups"),
            P(),
            P(("groups", "tok"), None, None),
            P(),
        ),
        out_specs=P(("groups", "tok"), None),
        check_vma=False,
    )
```
